256 devices in a mesh: depth: 2 (over core), lx: 16 (over y, x), ly: 8 (over z).
Axes of the slice: x: 4, y: 4, z: 8, core: 2. Of those that a mesh axis runs over, the one named last changes fastest.
Arguments:
- iterate: float32 [32, 4, 128, 1024], P('depth', None, 'lx', 'ly'), may hold values from -3 to 3
- right_side: float32 [32, 4, 128, 1024], P('depth', None, 'lx', 'ly'), may hold values from -64 to 64
- storage: float32 [32, 128, 1024], P('depth', 'lx', 'ly'), may hold values from 0.02 to 0.2
- zones: int32 [32, 128, 1024], P('depth', 'lx', 'ly'), may hold values from 0 to 7
- counts: int32 [128, 1024], P('lx', 'ly'), may hold values from 8 to 32
- materials: float32 [2, 8, 4, 4], replicated, as said below
Outputs:
- updated: float32 [32, 4, 128, 1024], P('depth', None, 'lx', 'ly')
- coarse: float32 [16, 4, 128, 1024], P('depth', None, 'lx', 'ly')
The draws below stay inside these ranges and needn't reach their ends.
Inputs may be any that keep to these rules, and one draw needn't show every extreme that they name: Nodes of column (x, y) with depth index below counts[x, y] are active. Each materials[t, k] is a symmetric matrix whose diagonal entries are positive and each larger than the sum of the magnitudes of the other entries in its row.
All inputs are finite; a program needn't handle non-finite values.
Results may differ from the reference program's by a relative error of at most 0.0003.
Values sent between devices are 32-bit elements; how exact they have to be, the bound alone decides.
A program may use at most 64 MiB of HBM per device.

```python
import math
import jax
import jax.numpy as jnp
from jax import lax

CZ = 16
CX = 8
CY = 128
COMP = 4
NZONE = 8
NZ = 32
NX = 128
NY = 1024
N_LX = 16
N_LY = 8


def draw_materials(key, part):
    key_diag, key_off = jax.random.split(jax.random.fold_in(key, 11))
    diagonal = jax.random.uniform(key_diag, (2, NZONE, 4), jnp.float32, 1.0, 1.6)
    coupling = jax.random.uniform(key_off, (2, NZONE, 4, 4), jnp.float32, -0.3, 0.3)
    coupling = 0.5 * (coupling + jnp.swapaxes(coupling, 2, 3))
    identity = jnp.eye(4, dtype=jnp.float32)
    matrix = coupling * (1.0 - identity) + diagonal[..., None] * identity
    scale = jnp.array([0.3, 64.0], jnp.float32)[:, None, None, None]
    return matrix * scale


def plant(result, own_key, least, top_value):
    extent = result.shape
    place = [jax.random.randint(jax.random.fold_in(own_key, axis), (), 0, extent[axis]) for axis in range(len(extent))]
    result = result.at[tuple(place)].set(least)
    longest = extent.index(max(extent))
    place[longest] = (place[longest] + 1) % extent[longest]
    return result.at[tuple(place)].set(top_value)


def block_levels(key, dims, cuts, least, top_value):
    def one(dim, shards_of):
        heights = jax.random.uniform(jax.random.fold_in(jax.random.fold_in(key, 6), dim), (shards_of,), jnp.float32, least / len(cuts), top_value / len(cuts))
        return jnp.repeat(jnp.exp(heights), dims[dim] // shards_of).reshape((-1,) + (1,) * (len(dims) - dim - 1))

    factor_of = one(*cuts[0])
    for cut in cuts[1:]:
        factor_of = factor_of * one(*cut)
    return factor_of


def bell_draw(stream_key, shape, width, limit, cuts=(), kind=jnp.bfloat16):
    values = jax.random.normal(stream_key, shape, jnp.float32) * width
    if len(cuts) > 0:
        values = block_levels(stream_key, shape, cuts, -0.22, 0.18) * values
    return jnp.clip(values, min=-limit, max=limit).astype(kind)


def setup_inputs(seed: int = 0) -> dict:
    arg_keys = jax.random.split(jax.random.key(seed), 7)
    iterate = bell_draw(arg_keys[0], (NZ, COMP, NX, NY), 0.5, 3.0, ((0, 2), (2, 16), (3, 8)), jnp.float32)
    right_side = bell_draw(arg_keys[1], (NZ, COMP, NX, NY), 10.0, 64.0, ((0, 2), (2, 16), (3, 8)), jnp.float32)
    storage = jnp.clip(jnp.exp(math.log(0.2) - 2.3025851 * jax.random.uniform(arg_keys[2], (NZ, NX, NY), jnp.float32) ** block_levels(arg_keys[2], (NZ, NX, NY), ((0, 2), (1, 16), (2, 8)), -0.2, 0.2)), 0.02, 0.2)
    zones = plant(jax.random.randint(arg_keys[3], (NZ, NX, NY), 0, NZONE), jax.random.fold_in(arg_keys[3], 1), 0, NZONE - 1).astype(jnp.int32)
    counts = plant(jax.random.randint(arg_keys[4], (NX, NY), CZ // 2, NZ + 1), jax.random.fold_in(arg_keys[4], 1), CZ // 2, NZ).astype(jnp.int32)
    materials = draw_materials(jax.random.fold_in(arg_keys[6], 71), 0)
    return {"iterate": iterate, "right_side": right_side, "storage": storage, "zones": zones, "counts": counts, "materials": materials}


def box_weights(values):
    values = 0.5 * values[:-2] + values[1:-1] + 0.5 * values[2:]
    values = 0.5 * values[..., :-2, :] + values[..., 1:-1, :] + 0.5 * values[..., 2:, :]
    return 0.5 * values[..., :-2] + values[..., 1:-1] + 0.5 * values[..., 2:]


def inner_part(values):
    return values[1:-1, ..., 1:-1, 1:-1]


def vertical_sum(values):
    return values[2:, ..., 1:-1, 1:-1] + values[:-2, ..., 1:-1, 1:-1]


def lateral_sum(values):
    return box_weights(values) - inner_part(values) - 0.5 * vertical_sum(values)


def lookup_table(weights, table):
    total = weights[0][:, None, None] * table[0][None, :, :, None, None]
    for index in range(1, len(weights)):
        total = total + weights[index][:, None, None] * table[index][None, :, :, None, None]
    return total


def block_apply(matrix, vector):
    total = matrix[..., :, 0, :, :] * vector[..., 0:1, :, :]
    for column in range(1, 4):
        total = total + matrix[..., :, column, :, :] * vector[..., column:column + 1, :, :]
    return total


def block_product(left, right):
    total = left[..., :, 0, :, :][..., :, None, :, :] * right[..., 0, :, :, :][..., None, :, :, :]
    for column in range(1, 4):
        total = total + left[..., :, column, :, :][..., :, None, :, :] * right[..., column, :, :, :][..., None, :, :, :]
    return total


def block_solve(matrix, right_part):
    rows = [[matrix[target, column] for column in range(4)] for target in range(4)]
    vectors = [right_part[target] for target in range(4)]
    for pivot_row in range(4):
        inverse = 1.0 / rows[pivot_row][pivot_row]
        for column in range(pivot_row + 1, 4):
            rows[pivot_row][column] = rows[pivot_row][column] * inverse
        vectors[pivot_row] = vectors[pivot_row] * inverse
        for target in range(4):
            if target != pivot_row:
                factor = rows[target][pivot_row]
                for column in range(pivot_row + 1, 4):
                    rows[target][column] = rows[target][column] - factor * rows[pivot_row][column]
                vectors[target] = vectors[target] - factor[None] * vectors[pivot_row]
    return jnp.stack(vectors)


def coefficients(codes_ext, materials, storage):
    zone_count = materials.shape[1]
    onehots = [(codes_ext == index + 1).astype(jnp.float32) for index in range(zone_count)]
    active_ext = (codes_ext > 0).astype(jnp.float32)
    lat_ext = lookup_table(onehots, materials[0])
    vert_ext = lookup_table(onehots, materials[1])
    lat_counts = [lateral_sum(item) for item in onehots]
    vert_counts = [vertical_sum(item) for item in onehots]
    lat_weight = lateral_sum(active_ext)
    vert_weight = vertical_sum(active_ext)
    active = inner_part(active_ext)
    beside_all = lookup_table(lat_counts, materials[0]) + lookup_table(vert_counts, materials[1])
    identity = jnp.eye(4, dtype=jnp.float32)[None, :, :, None, None]
    diagonal = storage[:, None, None] * identity + 0.5 * active[:, None, None] * (
        inner_part(lat_ext) * lat_weight[:, None, None] + inner_part(vert_ext) * vert_weight[:, None, None] + beside_all)
    column_codes = [item[:, 1:-1, 1:-1] for item in onehots]
    column_active = active_ext[:, 1:-1, 1:-1]
    link = column_active[:-1] * column_active[1:]
    pairs = 0.5 * lookup_table([(item[:-1] + item[1:]) * link for item in column_codes], materials[1])
    return active, active_ext, lat_ext, vert_ext, diagonal, pairs


def apply_operator(field_ext, coeffs):
    active, active_ext, lat_ext, vert_ext, diagonal, pairs = coeffs
    gated = field_ext * active_ext[:, None]
    lat_flow = block_apply(lat_ext, field_ext)
    vert_flow = block_apply(vert_ext, field_ext)
    off_part = block_apply(inner_part(lat_ext), lateral_sum(gated)) + lateral_sum(lat_flow)
    off_part = off_part + block_apply(inner_part(vert_ext), vertical_sum(gated)) + vertical_sum(vert_flow)
    return block_apply(diagonal, inner_part(field_ext)) - 0.5 * active[:, None] * off_part


def forward_sweep(diagonal, above, residual, carry_matrix, carry_columns):
    def advance(carry, level):
        coupled, columns = carry
        block, pair, value = level
        extra = jnp.concatenate([columns[:, :1] + value[:, None], columns[:, 1:]], axis=1)
        solved = block_solve(block - coupled, jnp.concatenate([pair, extra], axis=1))
        gain = solved[:, :4]
        rest = solved[:, 4:]
        return (block_product(pair, gain), block_product(pair, rest)), (gain, rest)

    (coupled, columns), (gains, rests) = lax.scan(advance, (carry_matrix, carry_columns), (diagonal, above, residual))
    return gains, rests, coupled, columns[:, 0]


def backward_sweep(gains, rests, incoming):
    def retreat(state, level):
        gain, rest = level
        width_gap = state.shape[1] - rest.shape[1]
        padding = jnp.zeros((4, width_gap) + rest.shape[2:], jnp.float32)
        state = jnp.concatenate([rest, padding], axis=1) + block_product(gain, state)
        return state, state

    return lax.scan(retreat, incoming, (gains, rests), reverse=True)[1]


def reference(iterate, right_side, storage, zones, counts, materials):
    depth_index = jnp.arange(NZ, dtype=jnp.int32)[:, None, None]
    codes = jnp.where(depth_index < counts[None], zones + 1, 0).astype(jnp.int32)
    codes_pad = jnp.pad(codes, 1)
    iterate_pad = jnp.pad(iterate, ((1, 1), (0, 0), (1, 1), (1, 1)))
    tiles = jnp.arange(N_LX * N_LY, dtype=jnp.int32)
    anchor = jnp.zeros((), jnp.int32)

    def tile_setup(tile):
        start_x = ((tile // N_LY) * CX).astype(jnp.int32)
        start_y = ((tile % N_LY) * CY).astype(jnp.int32)
        codes_ext = lax.dynamic_slice(codes_pad, (anchor, start_x, start_y), (NZ + 2, CX + 2, CY + 2))
        storage_tile = lax.dynamic_slice(storage, (anchor, start_x, start_y), (NZ, CX, CY))
        return start_x, start_y, coefficients(codes_ext, materials, storage_tile)

    def first_pass(tile):
        start_x, start_y, coeffs = tile_setup(tile)
        field_ext = lax.dynamic_slice(iterate_pad, (anchor, anchor, start_x, start_y), (NZ + 2, COMP, CX + 2, CY + 2))
        right_tile = lax.dynamic_slice(right_side, (anchor, anchor, start_x, start_y), (NZ, COMP, CX, CY))
        residual = coeffs[0][:, None] * (right_tile - apply_operator(field_ext, coeffs))
        gains, rests, coupled, vector = forward_sweep(coeffs[4], coeffs[5][1:], residual,
                                                      jnp.zeros((4, 4, CX, CY), jnp.float32),
                                                      jnp.zeros((4, 1, CX, CY), jnp.float32))
        states = backward_sweep(gains, rests, jnp.zeros((4, 1, CX, CY), jnp.float32))
        return residual, states[:, :, 0]

    def assemble(blocks):
        blocks = blocks.reshape(N_LX, N_LY, NZ, COMP, CX, CY)
        return blocks.transpose(2, 3, 0, 4, 1, 5).reshape(NZ, COMP, N_LX * CX, N_LY * CY)

    residual_tiles, correction_tiles = lax.map(first_pass, tiles)
    correction = assemble(correction_tiles)
    updated = iterate + correction
    correction_pad = jnp.pad(correction, ((1, 1), (0, 0), (1, 1), (1, 1)))

    def second_pass(inputs):
        tile, residual = inputs
        start_x, start_y, coeffs = tile_setup(tile)
        field_ext = lax.dynamic_slice(correction_pad, (anchor, anchor, start_x, start_y), (NZ + 2, COMP, CX + 2, CY + 2))
        return residual - apply_operator(field_ext, coeffs)

    smoothed = assemble(lax.map(second_pass, (tiles, residual_tiles)))
    odd_planes = smoothed[1::2]
    previous = jnp.concatenate([jnp.zeros_like(smoothed[:1]), odd_planes[:-1]], axis=0)
    coarse = 0.5 * previous + smoothed[0::2] + 0.5 * odd_planes
    return updated, coarse
```

```python
import functools

import jax
import jax.numpy as jnp
from jax import lax
from jax.experimental import pallas as pl
from jax.experimental.pallas import tpu as pltpu
from jax.sharding import PartitionSpec as P

F32 = jnp.float32
MESH = pl.DeviceIdType.MESH
Z = 16
SYM = [(i, j) for i in range(4) for j in range(i, 4)]
AT = {}
for _n, (_i, _j) in enumerate(SYM):
    AT[_i, _j] = _n
    AT[_j, _i] = _n


def sym_apply(m, v):
    out = []
    for i in range(4):
        a = m[AT[i, 0]] * v[0] + m[AT[i, 1]] * v[1]
        b = m[AT[i, 2]] * v[2] + m[AT[i, 3]] * v[3]
        out.append(a + b)
    return out


def sym_inverse(s, sa):
    def small(a, b, c, ra, rc):
        ca, cc = a * ra, c * rc
        q = 1.0 / (ca * cc - (b * ra) * (b * rc))
        return (cc * ra) * q, -((b * ra) * rc) * q, (ca * rc) * q

    a00, a01, a11 = small(s[AT[0, 0]], s[AT[0, 1]], s[AT[1, 1]], sa[0], sa[1])
    s02, s03, s12, s13 = s[AT[0, 2]], s[AT[0, 3]], s[AT[1, 2]], s[AT[1, 3]]
    e00, e01 = a00 * s02 + a01 * s12, a00 * s03 + a01 * s13
    e10, e11 = a01 * s02 + a11 * s12, a01 * s03 + a11 * s13
    c00 = s[AT[2, 2]] - (s02 * e00 + s12 * e10)
    c01 = s[AT[2, 3]] - (s02 * e01 + s12 * e11)
    c11 = s[AT[3, 3]] - (s03 * e01 + s13 * e11)
    x22, x23, x33 = small(c00, c01, c11, sa[2], sa[3])
    x02, x03 = -(e00 * x22 + e01 * x23), -(e00 * x23 + e01 * x33)
    x12, x13 = -(e10 * x22 + e11 * x23), -(e10 * x23 + e11 * x33)
    x00 = a00 - (x02 * e00 + x03 * e01)
    x01 = a01 - (x02 * e10 + x03 * e11)
    x11 = a11 - (x12 * e10 + x13 * e11)
    return [x00, x01, x02, x03, x11, x12, x13, x22, x23, x33]


def kernel(
    sizes,
    it_hbm, rhs_hbm, st_hbm, zn_hbm, ct_hbm, mat_hbm,
    up_hbm, co_hbm,
    mat, fi, rh, st, zn, ct, tab, cd, kl, mv, lk, gf, cf, up, sm, cu,
    inv, gain, sc, bv, rest,
    pk, sxc, sxi, sxd,
    rxc, rxi, rxd, ryc, ryi, ryd, rcc, rci, rcd,
    klx, kly, gx, gt, xt, yt,
    ifm_s, ifm_r, ifv_s, ifv_r, sm_r,
    ld_sem, out_sem, send, recv,
):
    n_lx, n_ly = sizes
    d = lax.axis_index("depth")
    x = lax.axis_index("lx")
    y = lax.axis_index("ly")
    o = 1 - d

    def near(dp, sx, sy):
        dd = d if dp == 0 else o
        return (dd, lax.rem(x + sx + n_lx, n_lx), lax.rem(y + sy + n_ly, n_ly))

    around = [(dp, sx, sy) for dp in (0, 1) for sx in (-1, 0, 1) for sy in (-1, 0, 1) if (dp, sx, sy) != (0, 0, 0)]

    loads = [
        pltpu.make_async_copy(zn_hbm, zn, ld_sem.at[0]),
        pltpu.make_async_copy(ct_hbm, ct, ld_sem.at[1]),
        pltpu.make_async_copy(it_hbm, fi.at[pl.ds(1, Z)], ld_sem.at[2]),
        pltpu.make_async_copy(st_hbm, st, ld_sem.at[3]),
        pltpu.make_async_copy(rhs_hbm, rh, ld_sem.at[4]),
    ]
    loads.append(pltpu.make_async_copy(mat_hbm, mat, ld_sem.at[5]))
    for item in loads:
        item.start()

    lane = lax.broadcasted_iota(jnp.int32, (8, 128), 1)
    row = lax.broadcasted_iota(jnp.int32, (8, 128), 0)
    zero = jnp.zeros((8, 128), F32)

    rxc[...] = jnp.zeros_like(rxc)
    rcc[...] = jnp.zeros_like(rcc)
    cd[pl.ds(17 * d, 1)] = jnp.zeros((1, 8, 128), F32)
    fi[pl.ds(17 * d, 1)] = jnp.zeros((1, 4, 8, 128), F32)
    cf[pl.ds(17 * d, 1)] = jnp.zeros((1, 4, 8, 128), F32)
    rxi[...] = jnp.zeros_like(rxi)
    rxd[...] = jnp.zeros_like(rxd)
    rci[...] = jnp.zeros_like(rci)
    rcd[...] = jnp.zeros_like(rcd)

    barrier = pltpu.get_barrier_semaphore()
    for place in around:
        pl.semaphore_signal(barrier, inc=1, device_id=near(*place), device_id_type=MESH)

    loads[5].wait()
    for kind in range(2):
        for n, (i, j) in enumerate(SYM):
            line = jnp.concatenate([mat[kind, i, pl.ds(j, 1), :], jnp.zeros((1, 120), F32)], axis=1)
            tab[kind * 10 + n] = pltpu.roll(jnp.broadcast_to(line, (8, 128)), 1, 1)

    loads[0].wait()
    loads[1].wait()
    count = ct[...]
    for z in range(Z):
        cd[z + 1] = jnp.where(z + Z * d < count, zn[z] + 1, 0).astype(F32)

    def pack_columns(ref, comps, first):
        total = zero
        for c in range(comps):
            acc = zero
            for z in range(Z):
                at = 32 * c + 2 * z
                v = ref[first + z, c] if comps > 1 else ref[first + z]
                v = pltpu.roll(v, at + 1, 1)
                acc = jnp.where((lane == at) | (lane == at + 1), v, acc)
            total = total + acc
        return total

    pk[0] = pack_columns(cd, 1, 1)
    for side in range(2):
        sxc[side] = cd[pl.ds(1, Z), 7 * side, :]

    loads[2].wait()
    pk[1] = pack_columns(fi, 4, 1)
    for c in range(4):
        for side in range(2):
            sxi[side, c] = fi[pl.ds(1, Z), c, 7 * side, :]

    pl.semaphore_wait(barrier, len(around))

    face = 15 * o
    far = 17 * d

    def copy(src, dst, n, who):
        return pltpu.make_async_remote_copy(
            src_ref=src, dst_ref=dst, send_sem=send.at[n], recv_sem=recv.at[n], device_id=who, device_id_type=MESH
        )

    def halo_copies(base, plane, pack, srow, rrow, ry, rc, comps):
        out = []

        def add(src, dst, who):
            out.append(copy(src, dst, base + len(out), who))

        for dp in (1, 0):
            for sx in (-1, 1):
                for sy in (-1, 1):
                    r = 7 if sx == 1 else 0
                    add(
                        pack.at[pl.ds(r, 1)],
                        rc.at[dp, 1 if sy == -1 else 0, pl.ds(r, 1)],
                        near(dp, sx, sy),
                    )
            for sy in (-1, 1):
                add(pack, ry.at[dp, 1 if sy == -1 else 0], near(dp, 0, sy))
            for sx in (-1, 1):
                s_side = 0 if sx == -1 else 1
                for c in range(comps):
                    src = srow.at[s_side, c] if comps > 1 else srow.at[s_side]
                    dst = rrow.at[1 - s_side, c] if comps > 1 else rrow.at[1 - s_side]
                    if dp == 1:
                        add(src.at[pl.ds(face, 1)], dst.at[pl.ds(far, 1)], near(1, sx, 0))
                    else:
                        add(src, dst.at[pl.ds(1, Z)], near(0, sx, 0))
        add(plane.at[pl.ds(face + 1, 1)], plane.at[pl.ds(far, 1)], near(1, 0, 0))
        return out

    code_copies = halo_copies(0, cd, pk.at[0], sxc, rxc, ryc, rcc, 1)
    for item in code_copies:
        item.start()
    field_copies = halo_copies(len(code_copies), fi, pk.at[1], sxi, rxi, ryi, rci, 4)
    for item in field_copies:
        item.start()
    used = len(code_copies) + len(field_copies)

    def lookup(code, kind):
        shape = code.shape
        index = code.astype(jnp.int32)
        out = []
        for n in range(10):
            parts = []
            for r in range(shape[0] // 8):
                parts.append(jnp.take_along_axis(tab[kind * 10 + n], index[8 * r : 8 * r + 8], axis=1))
            out.append(parts[0] if len(parts) == 1 else jnp.concatenate(parts, axis=0))
        return out

    def plane_coefficients(q):
        code = cd[q]
        values = lookup(code, 0)
        for n in range(10):
            kl[q, n] = values[n]
        kl[q, 10] = (code > 0).astype(F32)
        for n, v in enumerate(lookup(code, 1)):
            mv[q, n] = v

    def own_plane(z, _):
        plane_coefficients(z + 1)
        return 0

    lax.fori_loop(0, Z, own_plane, 0)
    for n in range(11):
        kl[17 * d, n] = zero
    for n in range(10):
        mv[17 * d, n] = zero

    def field_plane(src, q):
        act = kl[q, 10]
        v = [src[q, c] for c in range(4)]
        k = [kl[q, n] for n in range(10)]
        prod = sym_apply(k, v)
        for c in range(4):
            gf[q, c] = act * v[c]
            gf[q, 4 + c] = prod[c]

    def own_field(z, _):
        field_plane(fi, z + 1)
        return 0

    lax.fori_loop(0, Z, own_field, 0)

    for item in code_copies:
        item.wait_recv()

    near_plane = 17 * o
    plane_coefficients(near_plane)

    odd = (lane & 1) == 1
    other_at = 32 + 94 * d
    own_lane = lane < 32
    other_lane = (lane == other_at) | (lane == other_at + 1)

    def merge(ref, c):
        mine = jnp.where(odd, ref[0, 1], ref[0, 0])
        theirs = jnp.where(odd, ref[1, 1], ref[1, 0])
        if c > 0:
            mine = pltpu.roll(mine, 128 - 32 * c, 1)
        theirs = pltpu.roll(theirs, lax.rem(160 + 64 * d - 32 * c, 128), 1)
        return jnp.where(other_lane, theirs, jnp.where(own_lane, mine, 0.0))

    left_out = jnp.where(y == 0, 0, 1)
    right_out = jnp.where(y == n_ly - 1, 0, 1)
    below_out = jnp.where(x == 0, 0, 1)
    above_out = jnp.where(x == n_lx - 1, 0, 1)
    side_in = jnp.where(odd, right_out, left_out).astype(F32)
    corner_in = jnp.where(row == 7, below_out, above_out).astype(F32) * side_in
    for part, ref in ((0, ryc), (1, rcc)):
        code = merge(ref, 0) * (side_in if part == 0 else corner_in)
        values = lookup(code, 0)
        for n in range(10):
            kly[n, part] = values[n]
        kly[10, part] = (code > 0).astype(F32)
    for side in range(2):
        inside = (below_out if side == 0 else above_out).astype(F32)
        code = rxc[side] * inside
        values = lookup(code, 0)
        for n in range(10):
            klx[n, side] = values[n]
        klx[10, side] = (code > 0).astype(F32)

    def z_mix(v):
        return v + 0.5 * (pltpu.roll(v, 2, 1) + pltpu.roll(v, 126, 1))

    def around_rows(n, u, yc):
        u, yc = z_mix(u), z_mix(yc)
        hi = pltpu.roll(jnp.where(row == 7, yc, u), 1, 0)
        lo = pltpu.roll(jnp.where(row == 0, yc, u), 7, 0)
        yt[n] = u + 0.5 * (hi + lo)

    def row_sums(ref, n):
        for side in range(2):
            xt[n, side] = ref[n, side, pl.ds(1, Z), :] + 0.5 * (
                ref[n, side, pl.ds(0, Z), :] + ref[n, side, pl.ds(2, Z), :]
            )

    for n in range(11):
        around_rows(n, kly[n, 0], kly[n, 1])
        row_sums(klx, n)

    def lateral(ref, z, fields):
        mid = ref[z + 1, pl.ds(0, fields)] + 0.5 * (ref[z, pl.ds(0, fields)] + ref[z + 2, pl.ds(0, fields)])
        out = []
        for n in range(fields):
            v = mid[n]
            hi = jnp.where(row == 0, xt[n, 0, pl.ds(z, 1), :], pltpu.roll(v, 1, 0))
            lo = jnp.where(row == 7, xt[n, 1, pl.ds(z, 1), :], pltpu.roll(v, 7, 0))
            r = 0.5 * (hi + lo)
            s = v + r
            edge = pltpu.roll(yt[n], 127 - 2 * z, 1)
            left = pltpu.roll(jnp.where(lane == 127, edge, s), 1, 1)
            right = pltpu.roll(jnp.where(lane == 0, edge, s), 127, 1)
            out.append(r + 0.5 * (left + right))
        return out

    def couple(j):
        half = 0.5 * kl[j, 10] * kl[j + 1, 10]
        for n in range(10):
            mv[j, n] = half * (mv[j, n] + mv[j + 1, n])

    def couple_step(j, _):
        couple(j)
        return 0

    lax.fori_loop(0, 17, couple_step, 0)

    loads[3].wait()

    def block_step(z, _):
        sums = lateral(kl, z, 11)
        act = kl[z + 1, 10]
        half = 0.5 * act
        store = jnp.where(act > 0, st[z], 1.0)
        for n, (i, j) in enumerate(SYM):
            value = half * (kl[z + 1, n] * sums[10] + sums[n]) + (mv[z, n] + mv[z + 1, n])
            if i == j:
                value = value + store
                sc[z, i] = 1.0 / value
            lk[z, n] = value
        return 0

    lax.fori_loop(0, Z, block_step, 0)

    def place(t):
        return jnp.where(d == 0, t, 15 - t)

    def factor(s, scale, pair):
        xs = sym_inverse(s, scale)
        g = [[None] * 4 for _ in range(4)]
        for j in range(4):
            column = sym_apply(xs, [pair[AT[k, j]] for k in range(4)])
            for i in range(4):
                g[i][j] = column[i]
        nxt = []
        for i, j in SYM:
            a = pair[AT[i, 0]] * g[0][j] + pair[AT[i, 1]] * g[1][j]
            b = pair[AT[i, 2]] * g[2][j] + pair[AT[i, 3]] * g[3][j]
            nxt.append(a + b)
        return xs, g, nxt

    def chain(t, carry):
        z = place(t)
        s = [lk[z, n] - carry[n] for n in range(10)]
        xs, g, nxt = factor(s, [sc[z, i] for i in range(4)], [mv[z + o, n] for n in range(10)])
        for n in range(10):
            inv[z, n] = xs[n]
        for i in range(4):
            for j in range(4):
                gain[z, 4 * i + j] = g[i][j]
        for n in range(10):
            cu[n] = s[n]
        return tuple(nxt)

    last = lax.fori_loop(0, Z, chain, (zero,) * 10)
    for n in range(10):
        ifm_s[n] = last[n]
    matrix_copy = copy(ifm_s, ifm_r, used, near(1, 0, 0))
    matrix_copy.start()

    for item in field_copies:
        item.wait_recv()
    loads[4].wait()

    def halo_fields(rx, ry, rc):
        for part, ref in ((0, ry), (1, rc)):
            v = [merge(ref, c) for c in range(4)]
            prod = sym_apply([kly[n, part] for n in range(10)], v)
            for c in range(4):
                gt[c, part] = kly[10, part] * v[c]
                gt[4 + c, part] = prod[c]
        for side in range(2):
            v = [rx[side, c] for c in range(4)]
            prod = sym_apply([klx[n, side] for n in range(10)], v)
            for c in range(4):
                gx[c, side] = klx[10, side] * v[c]
                gx[4 + c, side] = prod[c]
        for n in range(8):
            around_rows(n, gt[n, 0], gt[n, 1])
            row_sums(gx, n)

    halo_fields(rxi, ryi, rci)
    field_plane(fi, 17 * d)
    field_plane(fi, near_plane)

    def neighbour_part(z):
        sums = lateral(gf, z, 8)
        half = 0.5 * kl[z + 1, 10]
        prod = sym_apply([kl[z + 1, n] for n in range(10)], sums[:4])
        return [half * (prod[c] + sums[4 + c]) for c in range(4)]

    def right_step(z, _):
        part = neighbour_part(z)
        on = kl[z + 1, 10] > 0
        for c in range(4):
            bv[z, c] = jnp.where(on, rh[z, c] + part[c], fi[z + 1, c])
        return 0

    lax.fori_loop(0, Z, right_step, 0)

    def forward(t, carry):
        z = place(t)
        v = [bv[z, c] + carry[c] for c in range(4)]
        r = sym_apply([inv[z, n] for n in range(10)], v)
        for c in range(4):
            rest[z, c] = r[c]
        g = [gain[z, n] for n in range(16)]
        out = []
        for i in range(4):
            out.append((g[i] * v[0] + g[4 + i] * v[1]) + (g[8 + i] * v[2] + g[12 + i] * v[3]))
        for c in range(4):
            bv[z, c] = v[c]
        return tuple(out)

    carried = lax.fori_loop(0, Z, forward, (zero,) * 4)
    for c in range(4):
        ifv_s[c] = carried[c]
    vector_copy = copy(ifv_s, ifv_r, used + 1, near(1, 0, 0))
    vector_copy.start()

    matrix_copy.wait_recv()
    end = place(15)
    closing = sym_inverse([cu[n] - ifm_r[n] for n in range(10)], [sc[end, i] for i in range(4)])
    vector_copy.wait_recv()
    u = sym_apply(closing, [bv[end, c] + ifv_r[c] for c in range(4)])

    def settle(z, values):
        for c in range(4):
            up[z, c] = values[c]
            cf[z + 1, c] = values[c] - fi[z + 1, c]

    settle(end, u)

    def backward(k, carry):
        z = place(14 - k)
        out = []
        for i in range(4):
            a = gain[z, 4 * i] * carry[0] + gain[z, 4 * i + 1] * carry[1]
            b = gain[z, 4 * i + 2] * carry[2] + gain[z, 4 * i + 3] * carry[3]
            out.append(rest[z, i] + (a + b))
        settle(z, out)
        return tuple(out)

    lax.fori_loop(0, Z - 1, backward, tuple(u))
    up_copy = pltpu.make_async_copy(up, up_hbm, out_sem.at[0])
    up_copy.start()

    pk[2] = pack_columns(cf, 4, 1)
    for c in range(4):
        for side in range(2):
            sxd[side, c] = cf[pl.ds(1, Z), c, 7 * side, :]
    change_copies = halo_copies(used + 2, cf, pk.at[2], sxd, rxd, ryd, rcd, 4)
    for item in change_copies:
        item.start()

    def own_change(z, _):
        field_plane(cf, z + 1)
        return 0

    lax.fori_loop(0, Z, own_change, 0)
    for item in change_copies:
        item.wait_recv()
    halo_fields(rxd, ryd, rcd)
    field_plane(cf, 17 * d)
    field_plane(cf, near_plane)

    def smooth_step(t, _):
        z = place(15 - t)
        part = neighbour_part(z)
        for c in range(4):
            sm[z, c] = part[c]
        return 0

    smooth_step(0, 0)
    top_copy = copy(sm.at[face], sm_r, used + 2 + len(change_copies), near(1, 0, 0))
    top_copy.start()
    lax.fori_loop(1, Z, smooth_step, 0)
    top_copy.wait_recv()

    from_below = jnp.where(d == 0, 0.0, 1.0)
    for k in range(Z // 2):
        for c in range(4):
            before = sm_r[c] * from_below if k == 0 else sm[2 * k - 1, c]
            cu[4 * k + c] = 0.5 * before + sm[2 * k, c] + 0.5 * sm[2 * k + 1, c]
    coarse_copies = []
    for k in range(Z // 2):
        coarse_copies.append(pltpu.make_async_copy(cu.at[pl.ds(4 * k, 4)], co_hbm.at[k], out_sem.at[1 + k]))
        coarse_copies[-1].start()
    for item in coarse_copies:
        item.wait()
    up_copy.wait()
    for item in code_copies + field_copies + [matrix_copy, vector_copy] + change_copies + [top_copy]:
        item.wait_send()


def local(sizes, iterate, right_side, storage, zones, counts, materials):
    V = pltpu.VMEM
    any_spec = pl.BlockSpec(memory_space=pl.ANY)
    blk = (8, 128)
    messages = 25 + 2 * 37 + 3
    shapes = [
        V((2, 4, 4, 8), F32),
        V((18, 4) + blk, F32),
        V((Z, 4) + blk, F32),
        V((Z,) + blk, F32),
        V((Z,) + blk, jnp.int32),
        V(blk, jnp.int32),
        V((20,) + blk, F32),
        V((18,) + blk, F32),
        V((18, 11) + blk, F32),
        V((18, 10) + blk, F32),
        V((Z, 10) + blk, F32),
        V((18, 8) + blk, F32),
        V((18, 4) + blk, F32),
        V((Z, 4) + blk, F32),
        V((Z, 4) + blk, F32),
        V((32,) + blk, F32),
        V((Z, 10) + blk, F32),
        V((Z, 16) + blk, F32),
        V((Z, 4) + blk, F32),
        V((Z, 4) + blk, F32),
        V((Z, 4) + blk, F32),
        V((3,) + blk, F32),
        V((2, Z, 128), F32),
        V((2, 4, Z, 128), F32),
        V((2, 4, Z, 128), F32),
        V((2, 24, 128), F32),
        V((2, 4, 24, 128), F32),
        V((2, 4, 24, 128), F32),
        V((2, 2) + blk, F32),
        V((2, 2) + blk, F32),
        V((2, 2) + blk, F32),
        V((2, 2) + blk, F32),
        V((2, 2) + blk, F32),
        V((2, 2) + blk, F32),
        V((11, 2, 24, 128), F32),
        V((11, 2) + blk, F32),
        V((8, 2, 24, 128), F32),
        V((8, 2) + blk, F32),
        V((11, 2, Z, 128), F32),
        V((11,) + blk, F32),
        V((10,) + blk, F32),
        V((10,) + blk, F32),
        V((4,) + blk, F32),
        V((4,) + blk, F32),
        V((4,) + blk, F32),
        pltpu.SemaphoreType.DMA((6,)),
        pltpu.SemaphoreType.DMA((9,)),
        pltpu.SemaphoreType.DMA((messages,)),
        pltpu.SemaphoreType.DMA((messages,)),
    ]
    return pl.pallas_call(
        functools.partial(kernel, sizes),
        out_shape=(
            jax.ShapeDtypeStruct((Z, 4) + blk, F32),
            jax.ShapeDtypeStruct((Z // 2, 4) + blk, F32),
        ),
        in_specs=[any_spec] * 6,
        out_specs=(any_spec, any_spec),
        scratch_shapes=shapes,
        compiler_params=pltpu.CompilerParams(collective_id=0, has_side_effects=True),
        name="zline",
    )(iterate, right_side, storage, zones, counts, jnp.transpose(materials, (0, 2, 3, 1)))


def solution(mesh):
    placed = (
        P("depth", None, "lx", "ly"),
        P("depth", None, "lx", "ly"),
        P("depth", "lx", "ly"),
        P("depth", "lx", "ly"),
        P("lx", "ly"),
        P(),
    )
    sizes = (mesh.shape["lx"], mesh.shape["ly"])
    return jax.shard_map(
        functools.partial(local, sizes),
        mesh=mesh,
        in_specs=placed,
        out_specs=(P("depth", None, "lx", "ly"), P("depth", None, "lx", "ly")),
        check_vma=False,
    )
```

```python
import functools

import jax
import jax.numpy as jnp
from jax import lax
from jax.experimental import pallas as pl
from jax.experimental.pallas import tpu as pltpu
from jax.sharding import PartitionSpec as P

F32 = jnp.float32
MESH = pl.DeviceIdType.MESH
Z = 16
SYM = [(i, j) for i in range(4) for j in range(i, 4)]
AT = {}
for _n, (_i, _j) in enumerate(SYM):
    AT[_i, _j] = _n
    AT[_j, _i] = _n


def face_rows(ref, comps, c, side):
    flat = ref.reshape(18 * comps * 8, 128)
    return flat[pl.ds(8 * comps + 8 * c + 7 * side, Z, stride=8 * comps), :]


def sym_apply(m, v):
    out = []
    for i in range(4):
        a = m[AT[i, 0]] * v[0] + m[AT[i, 1]] * v[1]
        b = m[AT[i, 2]] * v[2] + m[AT[i, 3]] * v[3]
        out.append(a + b)
    return out


def sym_inverse(s, sa):
    def small(a, b, c, ra, rc):
        ca, cc = a * ra, c * rc
        q = 1.0 / (ca * cc - (b * ra) * (b * rc))
        return (cc * ra) * q, -((b * ra) * rc) * q, (ca * rc) * q

    a00, a01, a11 = small(s[AT[0, 0]], s[AT[0, 1]], s[AT[1, 1]], sa[0], sa[1])
    s02, s03, s12, s13 = s[AT[0, 2]], s[AT[0, 3]], s[AT[1, 2]], s[AT[1, 3]]
    e00, e01 = a00 * s02 + a01 * s12, a00 * s03 + a01 * s13
    e10, e11 = a01 * s02 + a11 * s12, a01 * s03 + a11 * s13
    c00 = s[AT[2, 2]] - (s02 * e00 + s12 * e10)
    c01 = s[AT[2, 3]] - (s02 * e01 + s12 * e11)
    c11 = s[AT[3, 3]] - (s03 * e01 + s13 * e11)
    x22, x23, x33 = small(c00, c01, c11, sa[2], sa[3])
    x02, x03 = -(e00 * x22 + e01 * x23), -(e00 * x23 + e01 * x33)
    x12, x13 = -(e10 * x22 + e11 * x23), -(e10 * x23 + e11 * x33)
    x00 = a00 - (x02 * e00 + x03 * e01)
    x01 = a01 - (x02 * e10 + x03 * e11)
    x11 = a11 - (x12 * e10 + x13 * e11)
    return [x00, x01, x02, x03, x11, x12, x13, x22, x23, x33]


def kernel(
    sizes,
    it_hbm, rhs_hbm, st_hbm, zn_hbm, ct_hbm, mat_hbm,
    up_hbm, co_hbm,
    mat, fi, rh, st, zn, ct, tab, cd, kl, mv, lk, gf, cf, up, sm, cu,
    inv, gain, sc, bv, rest,
    pk, sxc, sxi, sxd,
    rxc, rxi, rxd, ryc, ryi, ryd, rcc, rci, rcd,
    klx, kly, gx, gt, xt, yt,
    ifm_s, ifm_r, ifv_s, ifv_r, sm_r,
    ld_sem, out_sem, send, recv,
):
    n_lx, n_ly = sizes
    d = lax.axis_index("depth")
    x = lax.axis_index("lx")
    y = lax.axis_index("ly")
    o = 1 - d

    def near(dp, sx, sy):
        dd = d if dp == 0 else o
        return (dd, x + sx, y + sy)

    def exists(sx, sy):
        tests = []
        if sx != 0:
            tests.append(x > 0 if sx < 0 else x < n_lx - 1)
        if sy != 0:
            tests.append(y > 0 if sy < 0 else y < n_ly - 1)
        if len(tests) == 2:
            return jnp.logical_and(*tests)
        return tests[0]

    ways = [(sx, sy) for sx in (-1, 0, 1) for sy in (-1, 0, 1) if (sx, sy) != (0, 0)]
    span_x = 3 - jnp.where(x == 0, 1, 0) - jnp.where(x == n_lx - 1, 1, 0)
    span_y = 3 - jnp.where(y == 0, 1, 0) - jnp.where(y == n_ly - 1, 1, 0)

    loads = [
        pltpu.make_async_copy(zn_hbm, zn, ld_sem.at[0]),
        pltpu.make_async_copy(ct_hbm, ct, ld_sem.at[1]),
        pltpu.make_async_copy(it_hbm, fi.at[pl.ds(1, Z)], ld_sem.at[2]),
        pltpu.make_async_copy(st_hbm, st, ld_sem.at[3]),
        pltpu.make_async_copy(rhs_hbm, rh, ld_sem.at[4]),
    ]
    loads.append(pltpu.make_async_copy(mat_hbm, mat, ld_sem.at[5]))
    for item in loads:
        item.start()

    lane = lax.broadcasted_iota(jnp.int32, (8, 128), 1)
    row = lax.broadcasted_iota(jnp.int32, (8, 128), 0)
    zero = jnp.zeros((8, 128), F32)

    for ref in (rxc, rcc, ryc, ryi, ryd):
        ref[...] = jnp.zeros_like(ref)
    cd[pl.ds(17 * d, 1)] = jnp.zeros((1, 8, 128), F32)
    fi[pl.ds(17 * d, 1)] = jnp.zeros((1, 4, 8, 128), F32)
    cf[pl.ds(17 * d, 1)] = jnp.zeros((1, 4, 8, 128), F32)
    rxi[...] = jnp.zeros_like(rxi)
    rxd[...] = jnp.zeros_like(rxd)
    rci[...] = jnp.zeros_like(rci)
    rcd[...] = jnp.zeros_like(rcd)

    barrier = pltpu.get_barrier_semaphore()
    pl.semaphore_signal(barrier, inc=1, device_id=near(1, 0, 0), device_id_type=MESH)
    for way in ways:

        @pl.when(exists(*way))
        def _():
            for dp in (0, 1):
                pl.semaphore_signal(barrier, inc=1, device_id=near(dp, *way), device_id_type=MESH)

    loads[5].wait()
    for kind in range(2):
        for n, (i, j) in enumerate(SYM):
            line = jnp.concatenate([mat[kind, i, pl.ds(j, 1), :], jnp.zeros((1, 120), F32)], axis=1)
            tab[kind * 10 + n] = pltpu.roll(jnp.broadcast_to(line, (8, 128)), 1, 1)

    loads[0].wait()
    loads[1].wait()
    count = ct[...]
    for z in range(Z):
        cd[z + 1] = jnp.where(z + Z * d < count, zn[z] + 1, 0).astype(F32)

    def pack_columns(ref, comps, first):
        total = zero
        for c in range(comps):
            acc = zero
            for z in range(Z):
                at = 32 * c + 2 * z
                v = ref[first + z, c] if comps > 1 else ref[first + z]
                v = pltpu.roll(v, at + 1, 1)
                acc = jnp.where((lane == at) | (lane == at + 1), v, acc)
            total = total + acc
        return total

    pk[0] = pack_columns(cd, 1, 1)
    for side in range(2):
        sxc[side] = face_rows(cd, 1, 0, side)

    loads[2].wait()
    pk[1] = pack_columns(fi, 4, 1)
    for c in range(4):
        for side in range(2):
            sxi[side, c] = face_rows(fi, 4, c, side)

    pl.semaphore_wait(barrier, 2 * span_x * span_y - 1)

    face = 15 * o
    far = 17 * d

    def copy(src, dst, n, who):
        return pltpu.make_async_remote_copy(
            src_ref=src, dst_ref=dst, send_sem=send.at[n], recv_sem=recv.at[n], device_id=who, device_id_type=MESH
        )

    class Halo:
        def __init__(self, base, plane, pack, srow, rrow, ry, rc, comps):
            every = (slice(None),) if comps > 1 else ()
            self.groups = {}
            for sx, sy in ways:
                group = []
                for dp in (1, 0):
                    n = base + 2 * ways.index((sx, sy)) + dp
                    side = 1 if sy == -1 else 0
                    if sx != 0 and sy != 0:
                        r = 7 if sx == 1 else 0
                        src, dst = pack.at[pl.ds(r, 1)], rc.at[dp, side, pl.ds(r, 1)]
                    elif sx == 0:
                        src, dst = pack, ry.at[dp, side]
                    else:
                        s_side = 0 if sx == -1 else 1
                        src, dst = srow.at[s_side], rrow.at[1 - s_side]
                        if dp == 1:
                            src, dst = src.at[every + (pl.ds(face, 1),)], dst.at[every + (pl.ds(far, 1),)]
                        else:
                            dst = dst.at[every + (pl.ds(1, Z),)]
                    group.append(copy(src, dst, n, near(dp, sx, sy)))
                self.groups[sx, sy] = group
            self.across = copy(plane.at[pl.ds(face + 1, 1)], plane.at[pl.ds(far, 1)], base + 16, near(1, 0, 0))

        def each(self, act, flip):
            act(self.across)
            for (sx, sy), group in self.groups.items():

                @pl.when(exists(flip * sx, flip * sy))
                def _():
                    for item in group:
                        act(item)

        def start(self):
            self.each(lambda item: item.start(), 1)

        def wait_recv(self):
            self.each(lambda item: item.wait_recv(), -1)

        def wait_send(self):
            self.each(lambda item: item.wait_send(), 1)

    code_halo = Halo(0, cd, pk.at[0], sxc, rxc, ryc, rcc, 1)
    code_halo.start()
    field_halo = Halo(17, fi, pk.at[1], sxi, rxi, ryi, rci, 4)
    field_halo.start()

    def lookup(code, kind):
        shape = code.shape
        index = code.astype(jnp.int32)
        out = []
        for n in range(10):
            parts = []
            for r in range(shape[0] // 8):
                parts.append(jnp.take_along_axis(tab[kind * 10 + n], index[8 * r : 8 * r + 8], axis=1))
            out.append(parts[0] if len(parts) == 1 else jnp.concatenate(parts, axis=0))
        return out

    def plane_coefficients(q):
        code = cd[q]
        values = lookup(code, 0)
        for n in range(10):
            kl[q, n] = values[n]
        kl[q, 10] = (code > 0).astype(F32)
        for n, v in enumerate(lookup(code, 1)):
            mv[q, n] = v

    def own_plane(z, _):
        plane_coefficients(z + 1)
        return 0

    lax.fori_loop(0, Z, own_plane, 0)
    for n in range(11):
        kl[17 * d, n] = zero
    for n in range(10):
        mv[17 * d, n] = zero

    def field_plane(src, q):
        act = kl[q, 10]
        v = [src[q, c] for c in range(4)]
        k = [kl[q, n] for n in range(10)]
        prod = sym_apply(k, v)
        for c in range(4):
            gf[q, c] = act * v[c]
            gf[q, 4 + c] = prod[c]

    def own_field(z, _):
        field_plane(fi, z + 1)
        return 0

    lax.fori_loop(0, Z, own_field, 0)

    code_halo.wait_recv()

    near_plane = 17 * o
    plane_coefficients(near_plane)

    odd = (lane & 1) == 1
    other_at = 32 + 94 * d
    own_lane = lane < 32
    other_lane = (lane == other_at) | (lane == other_at + 1)

    def merge(ref, c):
        mine = jnp.where(odd, ref[0, 1], ref[0, 0])
        theirs = jnp.where(odd, ref[1, 1], ref[1, 0])
        if c > 0:
            mine = pltpu.roll(mine, 128 - 32 * c, 1)
        theirs = pltpu.roll(theirs, lax.rem(160 + 64 * d - 32 * c, 128), 1)
        return jnp.where(other_lane, theirs, jnp.where(own_lane, mine, 0.0))

    for part, ref in ((0, ryc), (1, rcc)):
        code = merge(ref, 0)
        values = lookup(code, 0)
        for n in range(10):
            kly[n, part] = values[n]
        kly[10, part] = (code > 0).astype(F32)
    for side in range(2):
        code = rxc[side]
        values = lookup(code, 0)
        for n in range(10):
            klx[n, side] = values[n]
        klx[10, side] = (code > 0).astype(F32)

    def z_mix(v):
        return v + 0.5 * (pltpu.roll(v, 2, 1) + pltpu.roll(v, 126, 1))

    def around_rows(n, u, yc):
        u, yc = z_mix(u), z_mix(yc)
        hi = pltpu.roll(jnp.where(row == 7, yc, u), 1, 0)
        lo = pltpu.roll(jnp.where(row == 0, yc, u), 7, 0)
        yt[n] = u + 0.5 * (hi + lo)

    def row_sums(ref, n):
        for side in range(2):
            xt[n, side] = ref[n, side, pl.ds(1, Z), :] + 0.5 * (
                ref[n, side, pl.ds(0, Z), :] + ref[n, side, pl.ds(2, Z), :]
            )

    for n in range(11):
        around_rows(n, kly[n, 0], kly[n, 1])
        row_sums(klx, n)

    def lateral(ref, z, fields):
        mid = ref[z + 1, pl.ds(0, fields)] + 0.5 * (ref[z, pl.ds(0, fields)] + ref[z + 2, pl.ds(0, fields)])
        out = []
        for n in range(fields):
            v = mid[n]
            hi = jnp.where(row == 0, xt[n, 0, pl.ds(z, 1), :], pltpu.roll(v, 1, 0))
            lo = jnp.where(row == 7, xt[n, 1, pl.ds(z, 1), :], pltpu.roll(v, 7, 0))
            r = 0.5 * (hi + lo)
            s = v + r
            edge = pltpu.roll(yt[n], 127 - 2 * z, 1)
            left = pltpu.roll(jnp.where(lane == 127, edge, s), 1, 1)
            right = pltpu.roll(jnp.where(lane == 0, edge, s), 127, 1)
            out.append(r + 0.5 * (left + right))
        return out

    def couple(j):
        half = 0.5 * kl[j, 10] * kl[j + 1, 10]
        for n in range(10):
            mv[j, n] = half * (mv[j, n] + mv[j + 1, n])

    def couple_step(j, _):
        couple(j)
        return 0

    lax.fori_loop(0, 17, couple_step, 0)

    loads[3].wait()

    def block_step(z, _):
        sums = lateral(kl, z, 11)
        act = kl[z + 1, 10]
        half = 0.5 * act
        store = jnp.where(act > 0, st[z], 1.0)
        for n, (i, j) in enumerate(SYM):
            value = half * (kl[z + 1, n] * sums[10] + sums[n]) + (mv[z, n] + mv[z + 1, n])
            if i == j:
                value = value + store
                sc[z, i] = 1.0 / value
            lk[z, n] = value
        return 0

    lax.fori_loop(0, Z, block_step, 0)

    def place(t):
        return jnp.where(d == 0, t, 15 - t)

    def factor(s, scale, pair):
        xs = sym_inverse(s, scale)
        g = [[None] * 4 for _ in range(4)]
        for j in range(4):
            column = sym_apply(xs, [pair[AT[k, j]] for k in range(4)])
            for i in range(4):
                g[i][j] = column[i]
        nxt = []
        for i, j in SYM:
            a = pair[AT[i, 0]] * g[0][j] + pair[AT[i, 1]] * g[1][j]
            b = pair[AT[i, 2]] * g[2][j] + pair[AT[i, 3]] * g[3][j]
            nxt.append(a + b)
        return xs, g, nxt

    def chain(t, carry):
        z = place(t)
        s = [lk[z, n] - carry[n] for n in range(10)]
        xs, g, nxt = factor(s, [sc[z, i] for i in range(4)], [mv[z + o, n] for n in range(10)])
        for n in range(10):
            inv[z, n] = xs[n]
        for i in range(4):
            for j in range(4):
                gain[z, 4 * i + j] = g[i][j]
        for n in range(10):
            cu[n] = s[n]
        return tuple(nxt)

    last = lax.fori_loop(0, Z, chain, (zero,) * 10)
    for n in range(10):
        ifm_s[n] = last[n]
    matrix_copy = copy(ifm_s, ifm_r, 51, near(1, 0, 0))
    matrix_copy.start()

    field_halo.wait_recv()
    loads[4].wait()

    def halo_fields(rx, ry, rc):
        for part, ref in ((0, ry), (1, rc)):
            v = [merge(ref, c) for c in range(4)]
            prod = sym_apply([kly[n, part] for n in range(10)], v)
            for c in range(4):
                gt[c, part] = kly[10, part] * v[c]
                gt[4 + c, part] = prod[c]
        for side in range(2):
            v = [rx[side, c] for c in range(4)]
            prod = sym_apply([klx[n, side] for n in range(10)], v)
            for c in range(4):
                gx[c, side] = klx[10, side] * v[c]
                gx[4 + c, side] = prod[c]
        for n in range(8):
            around_rows(n, gt[n, 0], gt[n, 1])
            row_sums(gx, n)

    halo_fields(rxi, ryi, rci)
    field_plane(fi, 17 * d)
    field_plane(fi, near_plane)

    def neighbour_part(z):
        sums = lateral(gf, z, 8)
        half = 0.5 * kl[z + 1, 10]
        prod = sym_apply([kl[z + 1, n] for n in range(10)], sums[:4])
        return [half * (prod[c] + sums[4 + c]) for c in range(4)]

    def right_step(z, _):
        part = neighbour_part(z)
        on = kl[z + 1, 10] > 0
        for c in range(4):
            bv[z, c] = jnp.where(on, rh[z, c] + part[c], fi[z + 1, c])
        return 0

    lax.fori_loop(0, Z, right_step, 0)

    def forward(t, carry):
        z = place(t)
        v = [bv[z, c] + carry[c] for c in range(4)]
        r = sym_apply([inv[z, n] for n in range(10)], v)
        for c in range(4):
            rest[z, c] = r[c]
        g = [gain[z, n] for n in range(16)]
        out = []
        for i in range(4):
            out.append((g[i] * v[0] + g[4 + i] * v[1]) + (g[8 + i] * v[2] + g[12 + i] * v[3]))
        for c in range(4):
            bv[z, c] = v[c]
        return tuple(out)

    carried = lax.fori_loop(0, Z, forward, (zero,) * 4)
    for c in range(4):
        ifv_s[c] = carried[c]
    vector_copy = copy(ifv_s, ifv_r, 52, near(1, 0, 0))
    vector_copy.start()

    matrix_copy.wait_recv()
    end = place(15)
    closing = sym_inverse([cu[n] - ifm_r[n] for n in range(10)], [sc[end, i] for i in range(4)])
    vector_copy.wait_recv()
    u = sym_apply(closing, [bv[end, c] + ifv_r[c] for c in range(4)])

    def settle(z, values):
        for c in range(4):
            up[z, c] = values[c]
            cf[z + 1, c] = values[c] - fi[z + 1, c]

    settle(end, u)

    def backward(k, carry):
        z = place(14 - k)
        out = []
        for i in range(4):
            a = gain[z, 4 * i] * carry[0] + gain[z, 4 * i + 1] * carry[1]
            b = gain[z, 4 * i + 2] * carry[2] + gain[z, 4 * i + 3] * carry[3]
            out.append(rest[z, i] + (a + b))
        settle(z, out)
        return tuple(out)

    lax.fori_loop(0, Z - 1, backward, tuple(u))
    up_copy = pltpu.make_async_copy(up, up_hbm, out_sem.at[0])
    up_copy.start()

    pk[2] = pack_columns(cf, 4, 1)
    for c in range(4):
        for side in range(2):
            sxd[side, c] = face_rows(cf, 4, c, side)
    change_halo = Halo(34, cf, pk.at[2], sxd, rxd, ryd, rcd, 4)
    change_halo.start()

    def own_change(z, _):
        field_plane(cf, z + 1)
        return 0

    lax.fori_loop(0, Z, own_change, 0)
    change_halo.wait_recv()
    halo_fields(rxd, ryd, rcd)
    field_plane(cf, 17 * d)
    field_plane(cf, near_plane)

    def smooth_step(t, _):
        z = place(15 - t)
        part = neighbour_part(z)
        for c in range(4):
            sm[z, c] = part[c]
        return 0

    smooth_step(0, 0)
    top_copy = copy(sm.at[face], sm_r, 53, near(1, 0, 0))
    top_copy.start()
    lax.fori_loop(1, Z, smooth_step, 0)
    top_copy.wait_recv()

    from_below = jnp.where(d == 0, 0.0, 1.0)
    for k in range(Z // 2):
        for c in range(4):
            before = sm_r[c] * from_below if k == 0 else sm[2 * k - 1, c]
            cu[4 * k + c] = 0.5 * before + sm[2 * k, c] + 0.5 * sm[2 * k + 1, c]
    coarse_copies = []
    for k in range(Z // 2):
        coarse_copies.append(pltpu.make_async_copy(cu.at[pl.ds(4 * k, 4)], co_hbm.at[k], out_sem.at[1 + k]))
        coarse_copies[-1].start()
    for item in coarse_copies:
        item.wait()
    up_copy.wait()
    for item in (code_halo, field_halo, change_halo, matrix_copy, vector_copy, top_copy):
        item.wait_send()


def local(sizes, iterate, right_side, storage, zones, counts, materials):
    V = pltpu.VMEM
    any_spec = pl.BlockSpec(memory_space=pl.ANY)
    blk = (8, 128)
    messages = 3 * 17 + 3
    shapes = [
        V((2, 4, 4, 8), F32),
        V((18, 4) + blk, F32),
        V((Z, 4) + blk, F32),
        V((Z,) + blk, F32),
        V((Z,) + blk, jnp.int32),
        V(blk, jnp.int32),
        V((20,) + blk, F32),
        V((18,) + blk, F32),
        V((18, 11) + blk, F32),
        V((18, 10) + blk, F32),
        V((Z, 10) + blk, F32),
        V((18, 8) + blk, F32),
        V((18, 4) + blk, F32),
        V((Z, 4) + blk, F32),
        V((Z, 4) + blk, F32),
        V((32,) + blk, F32),
        V((Z, 10) + blk, F32),
        V((Z, 16) + blk, F32),
        V((Z, 4) + blk, F32),
        V((Z, 4) + blk, F32),
        V((Z, 4) + blk, F32),
        V((3,) + blk, F32),
        V((2, Z, 128), F32),
        V((2, 4, Z, 128), F32),
        V((2, 4, Z, 128), F32),
        V((2, 24, 128), F32),
        V((2, 4, 24, 128), F32),
        V((2, 4, 24, 128), F32),
        V((2, 2) + blk, F32),
        V((2, 2) + blk, F32),
        V((2, 2) + blk, F32),
        V((2, 2) + blk, F32),
        V((2, 2) + blk, F32),
        V((2, 2) + blk, F32),
        V((11, 2, 24, 128), F32),
        V((11, 2) + blk, F32),
        V((8, 2, 24, 128), F32),
        V((8, 2) + blk, F32),
        V((11, 2, Z, 128), F32),
        V((11,) + blk, F32),
        V((10,) + blk, F32),
        V((10,) + blk, F32),
        V((4,) + blk, F32),
        V((4,) + blk, F32),
        V((4,) + blk, F32),
        pltpu.SemaphoreType.DMA((6,)),
        pltpu.SemaphoreType.DMA((9,)),
        pltpu.SemaphoreType.DMA((messages,)),
        pltpu.SemaphoreType.DMA((messages,)),
    ]
    return pl.pallas_call(
        functools.partial(kernel, sizes),
        out_shape=(
            jax.ShapeDtypeStruct((Z, 4) + blk, F32),
            jax.ShapeDtypeStruct((Z // 2, 4) + blk, F32),
        ),
        in_specs=[any_spec] * 6,
        out_specs=(any_spec, any_spec),
        scratch_shapes=shapes,
        compiler_params=pltpu.CompilerParams(collective_id=0, has_side_effects=True),
        name="zline",
    )(iterate, right_side, storage, zones, counts, jnp.transpose(materials, (0, 2, 3, 1)))


def solution(mesh):
    placed = (
        P("depth", None, "lx", "ly"),
        P("depth", None, "lx", "ly"),
        P("depth", "lx", "ly"),
        P("depth", "lx", "ly"),
        P("lx", "ly"),
        P(),
    )
    sizes = (mesh.shape["lx"], mesh.shape["ly"])
    return jax.shard_map(
        functools.partial(local, sizes),
        mesh=mesh,
        in_specs=placed,
        out_specs=(P("depth", None, "lx", "ly"), P("depth", None, "lx", "ly")),
        check_vma=False,
    )
```
